32 devices in a mesh: dp: 8 (over y, x, core), head: 4 (over z).
Axes of the slice: x: 2, y: 2, z: 4, core: 2. Of those that a mesh axis runs over, the one named last changes fastest.
Arguments:
- stream: float32 [8192, 1024], P(('dp', 'head')), may hold values from -16 to 16
- cotangent: float32 [8192, 1024], P(('dp', 'head')), may hold values from -16 to 16
- documents: int32 [8, 1024], P('dp'), may hold values from 0 to 3, never falling along the last dimension, each value on 1 to 512 neighbouring positions
- attend_weight: bfloat16 [2, 3, 1024, 1024], P(None, None, None, 'head'), may hold values from -0.1875 to 0.1875
- output_weight: bfloat16 [2, 1024, 1024], P(None, 'head'), may hold values from -0.1875 to 0.1875
- expand_weight: bfloat16 [2, 2, 1024, 4096], P(None, None, None, 'head'), may hold values from -0.1875 to 0.1875
- reduce_weight: bfloat16 [2, 4096, 1024], P(None, 'head'), may hold values from -0.09375 to 0.09375
- score_gain: float32 [2, 1024], P(None, 'head'), may hold values from 0.8 to 1.6
- unit_gain: float32 [2, 2, 4096], P(None, None, 'head'), may hold values from 0.5 to 2
- alphas: float32 [2, 2, 1024], replicated, may hold values from 0.1 to 0.5
Outputs:
- result: float32 [8192, 1024], P(('dp', 'head'))
- stream_delta: float32 [8192, 1024], P(('dp', 'head'))
- attend_delta: float32 [2, 3, 1024, 1024], P(None, None, 'dp', 'head')
- output_delta: float32 [2, 1024, 1024], P(None, 'head', 'dp')
- expand_delta: float32 [2, 2, 1024, 4096], P(None, None, 'dp', 'head')
- reduce_delta: float32 [2, 4096, 1024], P(None, 'head', 'dp')
- score_delta: float32 [2, 1024], P(None, 'head')
- unit_delta: float32 [2, 2, 4096], P(None, None, 'head')
- alpha_delta: float32 [2, 2, 1024], replicated
- total_norm: float32 [], replicated
- alpha_mean: float32 [2, 2], replicated
The draws below stay inside these ranges and needn't reach their ends.
Inputs may be any that keep to these rules, and one draw needn't show every extreme that they name: `documents`: document numbers never fall along a sequence; a document holds at most 512 positions.
All inputs are finite; a program needn't handle non-finite values.
Results may differ from the reference program's by a relative error of at most 0.034.
Values may be sent and summed in bfloat16 or wider, within the bound.
No kernel may reach another device: no remote copies, remote signals or barrier semaphores. Data moves between devices by JAX's collectives and lax.ppermute only.
A program may use at most 256 MiB of HBM per device.

```python
import math
import jax
import jax.numpy as jnp
import numpy as np
from jax import lax

D = 1024
HEADS = 16
HDIM = 64
FF = 4096
LAYERS = 2
LEN = 1024
SEQS = 8
TOKENS = 8192


def column_field(key, low_end, high_end):
    columns = jnp.arange(D).astype(jnp.float32) / jnp.float32(D - 1)
    scales = low_end * jnp.exp(columns * jnp.log(jnp.float32(high_end / low_end)))
    values = jnp.clip(jax.random.normal(key, (TOKENS, D), jnp.float32), -6.0, 6.0)
    return values * scales[None, :]


def draw_stream(key, part):
    return column_field(jax.random.fold_in(key, 11), 0.6, 1.8)


def draw_cotangent(key, part):
    return column_field(jax.random.fold_in(key, 23), 0.6, 1.8)


def level_of(own_key, shape, split, smallest, top_value):
    def one(dim, shards_of):
        steps = jax.random.uniform(jax.random.fold_in(jax.random.fold_in(own_key, 6), dim), (shards_of,), jnp.float32, smallest / len(split), top_value / len(split))
        return jnp.repeat(jnp.exp(steps), shape[dim] // shards_of).reshape((-1,) + (1,) * (len(shape) - dim - 1))

    level = one(*split[0])
    for cut in split[1:]:
        level = level * one(*cut)
    return level


def split_up(count, total, most, slope):
    weights = [(1 << 20) // math.isqrt(rank ** slope) + 1 for rank in range(2, count + 1)]
    rest, holding = total - most - (count - 1), [1] * (count - 1)
    while rest > 0:
        movable = [i for i in range(count - 1) if holding[i] < most]
        mass, left = sum([weights[i] for i in movable]), rest
        for i in movable:
            more = min(most - holding[i], max(1, left * weights[i] // mass), rest)
            holding[i] = holding[i] + more
            rest = rest - more
    return np.array([most] + holding)


def ragged(key, number_of, total, limit, skew):
    if number_of == 2:
        one = jax.random.randint(key, (), max(1, total - limit), min(limit, total - 1) + 1)
        return jnp.stack([one, total - one])
    lengths = jnp.asarray(split_up(number_of, total, limit, skew), jnp.int32)
    twos = (number_of - 1) // 2
    donor, taker = lengths[1:1 + 2 * twos:2], lengths[2:2 + 2 * twos:2]
    margin = jnp.minimum(donor - 1, limit - taker)
    moved = jax.random.randint(jax.random.fold_in(key, 1), (twos,), 0, 1 << 20) % (margin + 1)
    lengths = lengths.at[1:1 + 2 * twos:2].set(donor - moved).at[2:2 + 2 * twos:2].set(taker + moved)
    return lengths[jax.random.permutation(jax.random.fold_in(key, 2), number_of)]


def gaussian(own_key, dims, deviation, reach, shards=(), kind=jnp.bfloat16):
    values = deviation * jax.random.normal(own_key, dims, jnp.float32)
    if shards:
        values = values * level_of(own_key, dims, shards, -0.22, 0.18)
    return jnp.clip(values, -reach, reach).astype(kind)


def setup_inputs(seed: int = 0) -> dict:
    key_of = jax.random.split(jax.random.key(seed), 11)
    stream = draw_stream(jax.random.fold_in(key_of[10], 71), 0)
    cotangent = draw_cotangent(jax.random.fold_in(key_of[10], 71), 0)
    documents = jax.vmap(lambda own: jnp.searchsorted(jnp.cumsum(ragged(own, 4, LEN, LEN // 2, 2)), jnp.arange(LEN), side="right"))(jax.random.split(key_of[2], SEQS)).reshape((SEQS, LEN)).astype(jnp.int32)
    attend_weight = gaussian(key_of[3], (LAYERS, 3, D, D), D ** -0.5, 0.1875, ((3, 4),))
    output_weight = gaussian(key_of[4], (LAYERS, D, D), D ** -0.5, 0.1875, ((1, 4),))
    expand_weight = gaussian(key_of[5], (LAYERS, 2, D, FF), D ** -0.5, 0.1875, ((3, 4),))
    reduce_weight = gaussian(key_of[6], (LAYERS, FF, D), FF ** -0.5, 0.09375, ((1, 4),))
    score_gain = jnp.clip(jnp.exp(math.log(1.6) - 0.6931472 * jax.random.uniform(key_of[7], (LAYERS, D), jnp.float32) ** level_of(key_of[7], (LAYERS, D), ((1, 4),), -0.2, 0.2)), 0.8, 1.6)
    unit_gain = jnp.clip(jnp.exp(math.log(2.0) - 1.3862944 * jax.random.uniform(key_of[8], (LAYERS, 2, FF), jnp.float32) ** level_of(key_of[8], (LAYERS, 2, FF), ((2, 4),), -0.2, 0.2)), 0.5, 2.0)
    alphas = jnp.clip(jnp.exp(jax.random.uniform(key_of[9], (LAYERS, 2, D), jnp.float32, math.log(0.1), math.log(0.5))), 0.1, 0.5)
    return dict(stream=stream, cotangent=cotangent, documents=documents, attend_weight=attend_weight, output_weight=output_weight, expand_weight=expand_weight, reduce_weight=reduce_weight, score_gain=score_gain, unit_gain=unit_gain, alphas=alphas)


@jax.custom_vjp
def low(v):
    return lax.optimization_barrier(v.astype(jnp.bfloat16)).astype(jnp.float32)

@jax.custom_vjp
def low_back(v):
    return v

def low_keep(v):
    return (low(v), None)

def low_pass(kept, grad):
    return (grad,)

def back_keep(v):
    return (v, None)

def back_low(kept, grad):
    return (low(grad),)
low.defvjp(low_keep, low_pass)
low_back.defvjp(back_keep, back_low)

def matmul(left, right):
    return jnp.dot(left, right, precision=lax.Precision.HIGHEST)

def sphere(values):
    return values * lax.rsqrt(lax.optimization_barrier(jnp.sum(values * values, axis=-1, keepdims=True)) + 1e-06)

def attend_sequence(inputs):
    queries, key_rows, values, labels = inputs
    logits = HDIM ** 0.5 * jnp.einsum('qhd,khd->hqk', queries, key_rows, precision=lax.Precision.HIGHEST)
    logits = low_back(logits)
    positions = jnp.arange(LEN)
    allowed = (positions[:, None] >= positions[None, :]) & (labels[:, None] == labels[None, :])
    scores = jnp.where(allowed[None], logits, -1e+30)
    attention = jax.nn.softmax(scores, axis=-1)
    return jnp.einsum('hqk,khd->qhd', low(attention), values, precision=lax.Precision.HIGHEST)

def one_layer(hidden, attend_weight, output_weight, expand_weight, reduce_weight, score_gain, unit_gain, alphas, documents):
    rounded = low(hidden)
    queries = low_back(matmul(rounded, attend_weight[0]))
    key_rows = low_back(matmul(rounded, attend_weight[1]))
    value_rows = low(low_back(matmul(rounded, attend_weight[2])))
    layout = (SEQS, LEN, HEADS, HDIM)
    scales = score_gain.reshape(HEADS, HDIM)
    query_unit = low(sphere(queries.reshape(layout)) * scales)
    key_unit = low(sphere(key_rows.reshape(layout)) * scales)
    context = lax.map(jax.checkpoint(attend_sequence), (query_unit, key_unit, value_rows.reshape(layout), documents))
    context = low(low_back(context.reshape(TOKENS, D)))
    branch = low_back(matmul(context, output_weight))
    hidden = sphere(hidden + alphas[0] * (sphere(branch) - hidden))
    rounded = low(hidden)
    up_part = low_back(matmul(rounded, expand_weight[0]))
    gate_part = low_back(matmul(rounded, expand_weight[1]))
    hidden_units = low(up_part * unit_gain[0] * jax.nn.silu(gate_part * unit_gain[1] * D ** 0.5))
    branch = low_back(matmul(hidden_units, reduce_weight))
    return sphere(hidden + alphas[1] * (sphere(branch) - hidden))

def reference(stream, cotangent, documents, attend_weight, output_weight, expand_weight, reduce_weight, score_gain, unit_gain, alphas):

    def forward(stream, attend_weight, output_weight, expand_weight, reduce_weight, score_gain, unit_gain, alphas):
        hidden = sphere(stream)
        for layer_index in range(LAYERS):
            hidden = one_layer(hidden, attend_weight[layer_index], output_weight[layer_index], expand_weight[layer_index], reduce_weight[layer_index], score_gain[layer_index], unit_gain[layer_index], alphas[layer_index], documents)
        return hidden
    result, pullback = jax.vjp(forward, stream, attend_weight.astype(jnp.float32), output_weight.astype(jnp.float32), expand_weight.astype(jnp.float32), reduce_weight.astype(jnp.float32), score_gain, unit_gain, alphas)
    gradients = pullback(cotangent)
    squares = jnp.float32(0.0)
    for entry in gradients[1:]:
        squares = squares + jnp.sum(entry * entry)
    total_norm = jnp.sqrt(squares)
    alpha_mean = lax.optimization_barrier(jnp.mean(alphas, axis=-1))
    return (result, gradients[0], gradients[1], gradients[2], gradients[3], gradients[4], gradients[5], gradients[6], gradients[7], total_norm, alpha_mean)
```

```python
import functools, math
import jax
import jax.numpy as jnp
from jax import lax
from jax.experimental import pallas as pl
from jax.experimental.pallas import tpu as pltpu
from jax.sharding import Mesh
from jax.sharding import PartitionSpec as P

D = 1024
HDIM = 64
BLOCK = 256
DOC_LIMIT = 512
SCALE = HDIM**0.5
EXP2_SCALE = SCALE * math.log2(math.e)
NT = (((1,), (1,)), ((), ()))
TN = (((0,), (0,)), ((), ()))
NN = (((1,), (0,)), ((), ()))


def mm(a, b, dims=NN):
    return lax.dot_general(a, b, dims, preferred_element_type=jnp.float32)


def head_lanes(shape, h):
    lanes = lax.broadcasted_iota(jnp.int32, shape, 1)
    return (lanes >= h * HDIM) & (lanes < (h + 1) * HDIM)


def reach(blocks):
    return min(blocks, -(-(DOC_LIMIT - 1) // BLOCK) + 1)


def by_window(i, blocks, run):
    most = reach(blocks)
    for n in range(1, most + 1):
        test = i == n - 1 if n < most else i >= n - 1
        pl.when(test)(functools.partial(run, n))


def attend_kernel(slot_ref, q_ref, k_ref, v_ref, rows_ref, cols_ref, ctx_ref, stat_ref):
    i = pl.program_id(0)
    width = q_ref.shape[1]

    def run(n):
        q = q_ref[...]
        doc_q = cols_ref[...]
        keys, values, masks = [], [], []
        for o in range(n):
            at = pl.ds(pl.multiple_of(slot_ref[i - o] * BLOCK, BLOCK), BLOCK)
            keys.append(k_ref[at, :])
            values.append(v_ref[at, :])
            doc_k = rows_ref[0:1, pl.ds(pl.multiple_of((i - o) * BLOCK, BLOCK), BLOCK)]
            seen = doc_q == doc_k
            if o == 0:
                shape = (BLOCK, BLOCK)
                seen = seen & (
                    lax.broadcasted_iota(jnp.int32, shape, 1)
                    <= lax.broadcasted_iota(jnp.int32, shape, 0)
                )
            masks.append(jnp.where(seen, 1.0, 0.0))
        context = jnp.zeros((BLOCK, width), jnp.float32)
        stats = jnp.zeros((BLOCK, 128), jnp.float32)
        for h in range(width // HDIM):
            mine = head_lanes((BLOCK, width), h)
            q_h = jnp.where(mine, q, jnp.zeros_like(q))
            total = None
            product = None
            for o in range(n):
                powers = jnp.exp2(mm(q_h, keys[o], NT) * EXP2_SCALE) * masks[o]
                part = jnp.sum(powers, axis=1, keepdims=True)
                term = mm(powers.astype(jnp.bfloat16), values[o])
                total = part if total is None else total + part
                product = term if product is None else product + term
            inverse = 1.0 / total
            context = jnp.where(mine, product * inverse, context)
            stats = jnp.where(
                lax.broadcasted_iota(jnp.int32, (BLOCK, 128), 1) == h, inverse, stats
            )
        ctx_ref[...] = context.astype(jnp.bfloat16)
        stat_ref[...] = stats.T[:8, :]

    by_window(i, k_ref.shape[0] // BLOCK, run)


def attend_forward(slots, q, k, v, rows, cols):
    length, width = q.shape
    blocks = length // BLOCK
    work = reach(blocks) * blocks * (width // HDIM) * 4 * BLOCK * BLOCK * width
    whole = pl.BlockSpec((length, width), lambda i, s: (0, 0))
    return pl.pallas_call(
        attend_kernel,
        out_shape=(
            jax.ShapeDtypeStruct((length, width), jnp.bfloat16),
            jax.ShapeDtypeStruct((8, length), jnp.float32),
        ),
        grid_spec=pltpu.PrefetchScalarGridSpec(
            num_scalar_prefetch=1,
            grid=(blocks,),
            in_specs=[
                pl.BlockSpec((BLOCK, width), lambda i, s: (s[i], 0)),
                whole,
                whole,
                pl.BlockSpec((8, length), lambda i, s: (0, 0)),
                pl.BlockSpec((BLOCK, 1), lambda i, s: (i, 0)),
            ],
            out_specs=[
                pl.BlockSpec((BLOCK, width), lambda i, s: (s[i], 0)),
                pl.BlockSpec((8, BLOCK), lambda i, s: (0, i)),
            ],
        ),
        compiler_params=pltpu.CompilerParams(dimension_semantics=("arbitrary",)),
        cost_estimate=pl.CostEstimate(
            flops=work, bytes_accessed=8 * length * width, transcendentals=0
        ),
    )(slots, q, k, v, rows, cols)


def attend_grad_kernel(
    slot_ref, q_ref, k_ref, v_ref, ctx_ref, grad_ref, rows_ref, cols_ref, stat_ref,
    dq_ref, dk_ref, dv_ref, dk_acc, dv_acc,
):
    i = pl.program_id(0)
    width = q_ref.shape[1]
    heads = width // HDIM

    def run(n):
        q = q_ref[...]
        grad = grad_ref[...]
        both = grad.astype(jnp.float32) * ctx_ref[...].astype(jnp.float32)
        high = both.astype(jnp.bfloat16)
        low = (both - high.astype(jnp.float32)).astype(jnp.bfloat16)
        pick_shape = (8, width)
        pick = jnp.where(
            lax.broadcasted_iota(jnp.int32, pick_shape, 1) // HDIM
            == lax.broadcasted_iota(jnp.int32, pick_shape, 0),
            1.0,
            0.0,
        ).astype(jnp.bfloat16)
        inner = mm(pick, high, NT) + mm(pick, low, NT)
        doc_q = rows_ref[0:1, :]
        spots, keys, values, masks = [], [], [], []
        for o in range(n):
            at = pl.ds(pl.multiple_of(slot_ref[i - o] * BLOCK, BLOCK), BLOCK)
            spots.append(at)
            keys.append(k_ref[at, :])
            values.append(v_ref[at, :])
            doc_k = cols_ref[pl.ds(pl.multiple_of((i - o) * BLOCK, BLOCK), BLOCK), :]
            seen = doc_q == doc_k
            if o == 0:
                shape = (BLOCK, BLOCK)
                seen = seen & (
                    lax.broadcasted_iota(jnp.int32, shape, 0)
                    <= lax.broadcasted_iota(jnp.int32, shape, 1)
                )
            masks.append(jnp.where(seen, 1.0, 0.0))
        dq = jnp.zeros((BLOCK, width), jnp.float32)
        dk = [None] * n
        dv = [None] * n
        for h in range(heads):
            mine = head_lanes((BLOCK, width), h)
            q_h = jnp.where(mine, q, jnp.zeros_like(q))
            grad_h = jnp.where(mine, grad, jnp.zeros_like(grad))
            inverse = stat_ref[h : h + 1, :]
            inner_h = inner[h : h + 1, :]
            dq_h = None
            for o in range(n):
                powers = jnp.exp2(mm(keys[o], q_h, NT) * EXP2_SCALE) * masks[o]
                probs = powers * inverse
                slope = (probs * (mm(values[o], grad_h, NT) - inner_h)).astype(jnp.bfloat16)
                term = mm(probs.astype(jnp.bfloat16), grad_h)
                dv[o] = term if dv[o] is None else dv[o] + term
                term = mm(slope, q_h)
                dk[o] = term if dk[o] is None else dk[o] + term
                term = mm(slope, keys[o], TN)
                dq_h = term if dq_h is None else dq_h + term
            dq = jnp.where(mine, dq_h, dq)
        dq_ref[...] = dq * SCALE
        for o in range(n):
            if o == 0:
                dk_acc[spots[o], :] = dk[o]
                dv_acc[spots[o], :] = dv[o]
            else:
                dk_acc[spots[o], :] += dk[o]
                dv_acc[spots[o], :] += dv[o]

    by_window(i, k_ref.shape[0] // BLOCK, run)

    @pl.when(i == pl.num_programs(0) - 1)
    def _():
        dk_ref[...] = dk_acc[...] * SCALE
        dv_ref[...] = dv_acc[...].astype(jnp.bfloat16)


def attend_backward(slots, q, k, v, ctx, grad, rows, cols, stats):
    length, width = q.shape
    blocks = length // BLOCK
    work = reach(blocks) * blocks * (width // HDIM) * 10 * BLOCK * BLOCK * width
    whole = pl.BlockSpec((length, width), lambda i, s: (0, 0))
    part = pl.BlockSpec((BLOCK, width), lambda i, s: (s[i], 0))
    return pl.pallas_call(
        attend_grad_kernel,
        out_shape=(
            jax.ShapeDtypeStruct((length, width), jnp.float32),
            jax.ShapeDtypeStruct((length, width), jnp.float32),
            jax.ShapeDtypeStruct((length, width), jnp.bfloat16),
        ),
        grid_spec=pltpu.PrefetchScalarGridSpec(
            num_scalar_prefetch=1,
            grid=(blocks,),
            in_specs=[
                part,
                whole,
                whole,
                part,
                part,
                pl.BlockSpec((8, BLOCK), lambda i, s: (0, i)),
                pl.BlockSpec((length, 1), lambda i, s: (0, 0)),
                pl.BlockSpec((8, BLOCK), lambda i, s: (0, i)),
            ],
            out_specs=[part, whole, whole],
            scratch_shapes=[
                pltpu.VMEM((length, width), jnp.float32),
                pltpu.VMEM((length, width), jnp.float32),
            ],
        ),
        compiler_params=pltpu.CompilerParams(dimension_semantics=("arbitrary",)),
        cost_estimate=pl.CostEstimate(
            flops=work, bytes_accessed=20 * length * width, transcendentals=0
        ),
    )(slots, q, k, v, ctx, grad, rows, cols, stats)


def sphere(values):
    return values * lax.rsqrt(jnp.sum(values * values, axis=-1, keepdims=True) + 1e-06)


def blend_unit(hidden, branch, mixing):
    return sphere(hidden + mixing * (sphere(branch) - hidden))


def gated_units(up_part, gate_part, up_gain, gate_gain):
    return up_part * up_gain * jax.nn.silu(gate_part * gate_gain * D**0.5)


def unit_heads(values, scales):
    heads_here = values.shape[1] // HDIM
    split = values.reshape(values.shape[0], heads_here, HDIM)
    return (sphere(split) * scales.reshape(heads_here, HDIM)).reshape(values.shape)


def flip(values, axis):
    return lax.ppermute(values, axis, [(0, 1), (1, 0)])


def trade(values):
    return lax.ppermute(values, ("core", "zh"), [(0, 0), (1, 2), (2, 1), (3, 3)])


def paired():
    return lax.axis_size("zl") == 2


def gather_rows(block):
    if not paired():
        return lax.all_gather(block, ("core", "zl"), axis=0, tiled=True)
    far = flip(block, "zl")
    near = flip(block, "core")
    return jnp.concatenate([block, near, far, flip(far, "core")])


def scatter_rows(product, local_rows):
    if not paired():
        return lax.psum_scatter(
            product.astype(jnp.bfloat16), ("core", "zl"), scatter_dimension=0, tiled=True
        ).astype(jnp.float32)
    own, near, far, cross = [
        product[n * local_rows : (n + 1) * local_rows] for n in range(4)
    ]
    low = jnp.bfloat16
    far_sum = far + flip(cross.astype(low), "core").astype(jnp.float32)
    near_sum = own + flip(near.astype(low), "core").astype(jnp.float32)
    return near_sum + flip(far_sum.astype(low), "zl").astype(jnp.float32)


def block_slots(length, local_rows):
    blocks = jnp.arange(length // BLOCK, dtype=jnp.int32)
    if not paired():
        return blocks
    per_slot = local_rows // BLOCK
    quarter = blocks // per_slot
    core = (quarter // 2) ^ lax.axis_index("core")
    side = (quarter % 2) ^ lax.axis_index("zl")
    return (side * 2 + core) * per_slot + blocks % per_slot


def fetch_weight(piece):
    return lax.all_gather(trade(piece), "xy", axis=0, tiled=True)


def own_part(values, axis, name):
    size = values.shape[axis] // lax.axis_size(name)
    return lax.dynamic_slice_in_dim(values, lax.axis_index(name) * size, size, axis)


def fetch_layer(attend_weight, output_weight, expand_weight, reduce_weight):
    rows = own_part(attend_weight, 1, "xy")
    columns = own_part(output_weight, 1, "xy")
    attend = fetch_weight(jnp.concatenate([rows[0], rows[1], rows[2], columns.T], axis=1))
    rows = own_part(expand_weight, 1, "xy")
    expand = fetch_weight(jnp.concatenate([rows[0], rows[1]], axis=1))
    return (attend, expand, fetch_weight(own_part(reduce_weight, 0, "xy")))


def return_gradient(part):
    piece = lax.psum_scatter(part, "xy", scatter_dimension=0, tiled=True)
    other = lax.ppermute(piece, ("core", "zh"), [(1, 0), (2, 3)])
    total = piece.astype(jnp.float32) + other.astype(jnp.float32)
    half = total.shape[0] // 2
    core = lax.axis_index("core")
    stay = lax.dynamic_slice_in_dim(total, core * half, half)
    leave = lax.dynamic_slice_in_dim(total, (1 - core) * half, half)
    moved = lax.ppermute(leave.astype(jnp.bfloat16), ("core", "zh"), [(0, 2), (3, 1)])
    return jnp.where(core == lax.axis_index("zh"), stay, moved.astype(jnp.float32))


def pair_lists(size):
    steps = []
    width = 1
    while width < size:
        steps.append([(n, n ^ width) for n in range(size)])
        width *= 2
    return steps


def add_over(values, axes):
    for axis in axes:
        for pairs in pair_lists(lax.axis_size(axis)):
            values = values + lax.ppermute(values, axis, pairs)
    return values


def rows_product(rows_low, grads_low):
    return lax.dot_general(rows_low, grads_low, TN, preferred_element_type=jnp.float32).astype(
        jnp.bfloat16
    )


def dot(left, right, dims=NN):
    return lax.dot_general(left, right, dims, preferred_element_type=jnp.float32)


def on_device(
    stream,
    cotangent,
    documents,
    attend_weight,
    output_weight,
    expand_weight,
    reduce_weight,
    score_gain,
    unit_gain,
    alphas,
):
    low = jnp.bfloat16
    local_rows = stream.shape[0]
    depth = attend_weight.shape[0]
    length = documents.shape[1]
    features = attend_weight.shape[3]
    units_here = reduce_weight.shape[1]
    weights = [None] * depth
    hidden = trade(sphere(stream).astype(low)).astype(jnp.float32)
    small = jnp.concatenate(
        [
            documents.reshape(-1).astype(jnp.float32),
            score_gain.reshape(-1),
            unit_gain.reshape(-1),
        ]
    ).reshape(-1, 128)
    small = trade(small).reshape(-1)
    labels = small[: documents.size].reshape(documents.shape)
    score_gain = small[documents.size : documents.size + score_gain.size].reshape(
        score_gain.shape
    )
    unit_gain = small[documents.size + score_gain.size :].reshape(unit_gain.shape)
    doc_rows = jnp.broadcast_to(labels.reshape(1, -1), (8, labels.size))
    doc_columns = labels.reshape(-1, 1)
    slots = block_slots(length, local_rows)
    for layer in range(depth):
        weights[layer] = fetch_layer(
            attend_weight[layer], output_weight[layer], expand_weight[layer], reduce_weight[layer]
        )
    flowing = trade(cotangent.astype(low)).astype(jnp.float32)
    records = []
    for layer in range(depth):
        attend, expand, reduce = weights[layer]
        attend_rows = gather_rows(hidden.astype(low))
        queries = dot(attend_rows, attend[:, :features])
        key_rows = dot(attend_rows, attend[:, features : 2 * features])
        value_rows = dot(attend_rows, attend[:, 2 * features : 3 * features]).astype(low)
        query_unit = unit_heads(queries, score_gain[layer]).astype(low)
        key_unit = unit_heads(key_rows, score_gain[layer]).astype(low)
        context, stats = attend_forward(
            slots, query_unit, key_unit, value_rows, doc_rows, doc_columns
        )
        branch = scatter_rows(dot(context, attend[:, 3 * features :], NT), local_rows)
        middle = blend_unit(hidden, branch, alphas[layer, 0])
        expand_rows = gather_rows(middle.astype(low))
        up_part = dot(expand_rows, expand[:, :units_here])
        gate_part = dot(expand_rows, expand[:, units_here:])
        units = gated_units(up_part, gate_part, unit_gain[layer, 0], unit_gain[layer, 1]).astype(
            low
        )
        reduced = scatter_rows(dot(units, reduce), local_rows)
        records.append(
            (
                hidden,
                middle,
                branch,
                reduced,
                attend_rows,
                expand_rows,
                queries,
                key_rows,
                query_unit,
                key_unit,
                value_rows,
                context,
                stats,
                up_part,
                gate_part,
                units,
            )
        )
        hidden = blend_unit(middle, reduced, alphas[layer, 1])
    result = trade(hidden.astype(low)).astype(jnp.float32)
    weight_parts = [None] * depth
    score_parts = [None] * depth
    unit_parts = [None] * depth
    alpha_parts = [None] * depth
    for layer in range(depth - 1, -1, -1):
        (
            before,
            middle,
            branch,
            reduced,
            attend_rows,
            expand_rows,
            queries,
            key_rows,
            query_unit,
            key_unit,
            value_rows,
            context,
            stats,
            up_part,
            gate_part,
            units,
        ) = records[layer]
        attend, expand, reduce = weights[layer]
        unused, pullback = jax.vjp(blend_unit, middle, reduced, alphas[layer, 1])
        middle_grad, reduced_grad, alpha_second = pullback(flowing)
        reduced_full = gather_rows(reduced_grad.astype(low))
        units_grad = dot(reduced_full, reduce, NT)
        reduce_part = return_gradient(rows_product(reduced_full, units))
        unused, pull_gate = jax.vjp(
            gated_units, up_part, gate_part, unit_gain[layer, 0], unit_gain[layer, 1]
        )
        up_grad, gate_grad, up_gain_grad, gate_gain_grad = pull_gate(units_grad)
        pair_low = jnp.concatenate([up_grad.astype(low), gate_grad.astype(low)], axis=1)
        middle_grad = middle_grad + scatter_rows(dot(pair_low, expand, NT), local_rows)
        expand_part = return_gradient(rows_product(expand_rows, pair_low))
        unused, pullback = jax.vjp(blend_unit, before, branch, alphas[layer, 0])
        hidden_grad, branch_grad, alpha_first = pullback(middle_grad)
        branch_full = gather_rows(branch_grad.astype(low))
        context_grad = dot(branch_full, attend[:, 3 * features :]).astype(low)
        query_unit_grad, key_unit_grad, value_low = attend_backward(
            slots,
            query_unit,
            key_unit,
            value_rows,
            context,
            context_grad,
            doc_rows,
            doc_columns,
            stats,
        )
        unused, pull_query = jax.vjp(unit_heads, queries, score_gain[layer])
        query_grad, query_gain = pull_query(query_unit_grad)
        unused, pull_key = jax.vjp(unit_heads, key_rows, score_gain[layer])
        key_grad, key_gain = pull_key(key_unit_grad)
        triple_low = jnp.concatenate(
            [query_grad.astype(low), key_grad.astype(low), value_low], axis=1
        )
        flowing = hidden_grad + scatter_rows(
            dot(triple_low, attend[:, : 3 * features], NT), local_rows
        )
        attend_part = return_gradient(
            jnp.concatenate(
                [rows_product(attend_rows, triple_low), rows_product(branch_full, context)], axis=1
            )
        )
        weight_parts[layer] = (attend_part, expand_part, reduce_part)
        score_parts[layer] = query_gain + key_gain
        unit_parts[layer] = jnp.stack([up_gain_grad, gate_gain_grad])
        alpha_parts[layer] = jnp.stack([alpha_first, alpha_second])
    unused, pullback = jax.vjp(sphere, stream)
    stream_delta = pullback(trade(flowing.astype(low)).astype(jnp.float32))[0]
    score_parts = jnp.stack(score_parts)
    unit_parts = jnp.stack(unit_parts)
    alpha_parts = jnp.stack(alpha_parts)
    vector = jnp.concatenate(
        [score_parts.reshape(-1), unit_parts.reshape(-1), alpha_parts.reshape(-1)]
    ).reshape(-1, 128)
    vector = add_over(vector, ("xy", "zh"))
    cut = (score_parts.size + unit_parts.size) // 128
    mine = trade(vector[:cut]).reshape(-1)
    alpha_delta = add_over(vector[cut:], ("core", "zl")).reshape(alpha_parts.shape)
    score_delta = mine[: score_parts.size].reshape(score_parts.shape)
    unit_delta = mine[score_parts.size :].reshape(unit_parts.shape)
    attend_delta = jnp.stack(
        [
            jnp.stack(
                [part[0][:, n * features : (n + 1) * features] for n in range(3)]
            )
            for part in weight_parts
        ]
    )
    output_delta = jnp.stack([part[0][:, 3 * features :].T for part in weight_parts])
    expand_delta = jnp.stack(
        [
            jnp.stack([part[1][:, :units_here], part[1][:, units_here:]])
            for part in weight_parts
        ]
    )
    reduce_delta = jnp.stack([part[2].T for part in weight_parts])
    squares = jnp.float32(0.0)
    for part in weight_parts:
        for entry in part:
            squares = squares + jnp.sum(entry * entry)
    rows_of = lax.axis_size("xy") * lax.axis_size("core")
    squares = squares + (
        jnp.sum(score_delta * score_delta) + jnp.sum(unit_delta * unit_delta)
    ) / rows_of
    squares = squares + jnp.sum(alpha_delta * alpha_delta) / (
        rows_of * lax.axis_size("zh") * lax.axis_size("zl")
    )
    squares = add_over(
        jnp.broadcast_to(squares, (8, 128)), ("core", "zl", "zh", "xy")
    )
    total_norm = jnp.sqrt(squares[0, 0])
    alpha_mean = jnp.mean(alphas, axis=-1)
    return (
        result,
        stream_delta,
        attend_delta,
        output_delta,
        expand_delta,
        reduce_delta,
        score_delta,
        unit_delta,
        alpha_delta,
        total_norm,
        alpha_mean,
    )


def solution(mesh):
    dp = ("xy", "core")
    head = ("zh", "zl")
    groups, lines = mesh.devices.shape
    inner = Mesh(
        mesh.devices.reshape(groups // 2, 2, 2, lines // 2), ("xy", "core", "zh", "zl")
    )
    return jax.shard_map(
        on_device,
        mesh=inner,
        in_specs=(
            P(dp + head, None),
            P(dp + head, None),
            P(dp, None),
            P(None, None, None, head),
            P(None, head, None),
            P(None, None, None, head),
            P(None, head, None),
            P(None, head),
            P(None, None, head),
            P(),
        ),
        out_specs=(
            P(dp + head, None),
            P(dp + head, None),
            P(None, None, dp, head),
            P(None, head, dp),
            P(None, None, dp, head),
            P(None, head, dp),
            P(None, head),
            P(None, None, head),
            P(),
            P(),
            P(),
        ),
        check_vma=False,
    )
```
